1024 devices in a mesh: dp: 2 (over x_hi), outer: 128 (over z, x_lo, core), inner: 4 (over y).
Axes of the slice: x: 4 (x_hi: 2, x_lo: 2; x = x_hi * 2 + x_lo), y: 4, z: 32, core: 2. Of those that a mesh axis runs over, the one named last changes fastest.
Arguments:
- queries: bfloat16 [65536, 4096], P(('outer', 'inner'), 'dp'), may hold values from -512 to 512
- out_grad: bfloat16 [65536, 4096], P(('outer', 'inner'), 'dp'), may hold values from -6 to 6
- key_rows: bfloat16 [65536, 512], P(('outer', 'inner')), may hold values from -14 to 14
- value_rows: bfloat16 [65536, 512], P(('outer', 'inner')), may hold values from -6 to 6
- block_order: int32 [512], replicated, may hold values from 0 to 511, each once
- block_flags: int32 [512, 5], replicated, may hold values 0 or 1
Outputs:
- query_grad: bfloat16 [65536, 4096], P(('outer', 'inner'), 'dp')
- key_grad: float32 [65536, 512], P(('outer', 'inner'), 'dp')
- value_grad: float32 [65536, 512], P(('outer', 'inner'), 'dp')
The draws below stay inside these ranges and needn't reach their ends.
Inputs may be any that keep to these rules, and one draw needn't show every extreme that they name: `block_order`: each number appears once.
All inputs are finite; a program needn't handle non-finite values.
Results may differ from the reference program's by a relative error of at most 0.005.
Values may be sent and summed in bfloat16 or wider, within the bound.
No kernel may reach another device: no remote copies, remote signals or barrier semaphores. Data moves between devices by JAX's collectives and lax.ppermute only.
A program may use at most 32 MiB of HBM per device.

```python
import math
import jax
import jax.numpy as jnp
from jax import lax

HEADS = 32
KV_HEADS = 4
HD = 128
ROWS = 128
SHARDS = 512
SLOTS = 5
TOKENS = 65536
N_OUTER = 128
N_INNER = 4


def shared_keys(key):
    base_draw = jnp.clip(jax.random.normal(jax.random.fold_in(key, 7), (TOKENS, KV_HEADS, HD), jnp.float32), -4.5, 4.5)
    return base_draw


def draw_key_rows(key, part):
    key_draw = shared_keys(key)
    return key_draw.reshape(TOKENS, KV_HEADS * HD).astype(jnp.bfloat16)


def draw_queries(key, part):
    raw_draw = jnp.clip(jax.random.normal(jax.random.fold_in(key, 11), (TOKENS, HEADS // KV_HEADS, KV_HEADS, HD), jnp.float32), -4.5, 4.5)
    return raw_draw.reshape(TOKENS, HEADS * HD).astype(jnp.bfloat16)


def touch_ends(entries, stream_key, smallest, high):
    spot = [jax.random.randint(jax.random.fold_in(stream_key, axis), (), 0, length) for axis, length in enumerate(entries.shape)]
    longest = entries.shape.index(max(entries.shape))
    beside = spot[:longest] + [(spot[longest] + 1) % entries.shape[longest]] + spot[longest + 1:]
    return entries.at[tuple(spot)].set(smallest).at[tuple(beside)].set(high)


def block_levels(key, shape, pieces, smallest, top_value):
    loudness, own = 1.0, jax.random.fold_in(key, 6)
    for axis_at, shards_of in pieces:
        steps = jnp.exp(jax.random.uniform(jax.random.fold_in(own, axis_at), (shards_of,), jnp.float32, smallest / len(pieces), top_value / len(pieces)))
        loudness = loudness * jnp.repeat(steps, shape[axis_at] // shards_of).reshape([-1 if axis == axis_at else 1 for axis in range(len(shape))])
    return loudness


def gaussian(stream_key, shape, spread, bound, pieces=(), held_as=jnp.bfloat16):
    entries = jax.random.normal(stream_key, shape, jnp.float32) * spread
    if len(pieces) > 0:
        entries = block_levels(stream_key, shape, pieces, -0.22, 0.18) * entries
    return jnp.clip(entries, min=-bound, max=bound).astype(held_as)


def setup_inputs(seed: int = 0) -> dict:
    key_of = jax.random.split(jax.random.key(seed), 7)
    return {
        "queries": draw_queries(jax.random.fold_in(key_of[6], 71), 0),
        "out_grad": gaussian(key_of[1], (TOKENS, HEADS * HD), 1.0, 6.0, ((0, 512), (1, 2))),
        "key_rows": draw_key_rows(jax.random.fold_in(key_of[6], 71), 0),
        "value_rows": gaussian(key_of[3], (TOKENS, KV_HEADS * HD), 1.0, 6.0, ((0, 512),)),
        "block_order": jax.random.permutation(key_of[4], SHARDS).astype(jnp.int32),
        "block_flags": touch_ends((jax.random.randint(key_of[5], (SHARDS, SLOTS), 0, 4) < 3).astype(jnp.int32), jax.random.fold_in(key_of[5], 1), 0, 1),
    }


def window_grads(query_block, grad_block, key_window, value_window, visible, score_scale):
    query_wide = query_block.astype(jnp.float32)
    grad_wide = grad_block.astype(jnp.float32)
    key_wide = key_window.astype(jnp.float32)
    value_wide = value_window.astype(jnp.float32)
    seen = visible[:, None, None, :]
    scores = jnp.einsum('rgjd,wjd->rgjw', query_wide, key_wide) * score_scale
    row_max = lax.optimization_barrier(jnp.max(jnp.where(seen, scores, -jnp.inf), axis=-1, keepdims=True))
    exp_scores = jnp.where(seen, jnp.exp(scores - row_max), 0.0)
    soft_weights = exp_scores / lax.optimization_barrier(jnp.sum(exp_scores, axis=-1, keepdims=True))
    soft_low = lax.optimization_barrier(soft_weights.astype(jnp.bfloat16)).astype(jnp.float32)
    weight_grads = jnp.einsum('rgjd,wjd->rgjw', grad_wide, value_wide)
    row_delta = lax.optimization_barrier(jnp.sum(soft_weights * weight_grads, axis=-1, keepdims=True))
    score_grads = (soft_weights * (weight_grads - row_delta) * score_scale).astype(jnp.bfloat16)
    score_wide = lax.optimization_barrier(score_grads).astype(jnp.float32)
    query_part = jnp.einsum('rgjw,wjd->rgjd', score_wide, key_wide).astype(jnp.bfloat16)
    key_part = jnp.einsum('rgjw,rgjd->wjd', score_wide, query_wide)
    value_part = jnp.einsum('rgjw,rgjd->wjd', soft_low, grad_wide)
    return (query_part, key_part, value_part)

def reference(queries, out_grad, key_rows, value_rows, block_order, block_flags):
    score_scale = 1.0 / math.sqrt(HD)
    group_count = HEADS // KV_HEADS
    shard_total = N_OUTER * N_INNER
    query_shards = queries.reshape(shard_total, ROWS, group_count, KV_HEADS, HD)
    grad_shards = out_grad.reshape(shard_total, ROWS, group_count, KV_HEADS, HD)
    key_table = key_rows.reshape(TOKENS, KV_HEADS, HD)
    value_table = value_rows.reshape(TOKENS, KV_HEADS, HD)
    row_index = jnp.arange(ROWS, dtype=jnp.int32)
    positions = (block_order[:, None] * ROWS + row_index[None, :]).astype(jnp.int32)
    slot_index = jnp.arange(N_INNER + 1, dtype=jnp.int32)
    group_span = N_INNER * ROWS

    def step(totals, shard_index):
        key_total, value_total = totals
        outer_index = shard_index // N_INNER
        member_index = shard_index % N_INNER
        previous = (outer_index + N_OUTER - 1) % N_OUTER * N_INNER + member_index
        group_start = (outer_index * group_span).astype(jnp.int32)
        prev_start = (previous * ROWS).astype(jnp.int32)
        key_window = jnp.concatenate([lax.dynamic_slice_in_dim(key_table, group_start, group_span, 0), lax.dynamic_slice_in_dim(key_table, prev_start, ROWS, 0)], 0)
        value_window = jnp.concatenate([lax.dynamic_slice_in_dim(value_table, group_start, group_span, 0), lax.dynamic_slice_in_dim(value_table, prev_start, ROWS, 0)], 0)
        group_pos = lax.dynamic_slice_in_dim(positions, (outer_index * N_INNER).astype(jnp.int32), N_INNER, 0).reshape(-1)
        key_pos = jnp.concatenate([group_pos, positions[previous]], 0)
        allowed = (block_flags[shard_index] == 1) | (slot_index == member_index)
        visible = (key_pos[None, :] <= positions[shard_index][:, None]) & jnp.repeat(allowed, ROWS)[None, :]
        query_part, key_part, value_part = window_grads(query_shards[shard_index], grad_shards[shard_index], key_window, value_window, visible, score_scale)
        key_total = lax.dynamic_update_slice_in_dim(key_total, lax.dynamic_slice_in_dim(key_total, group_start, group_span, 0) + key_part[:group_span], group_start, 0)
        key_total = lax.dynamic_update_slice_in_dim(key_total, lax.dynamic_slice_in_dim(key_total, prev_start, ROWS, 0) + key_part[group_span:], prev_start, 0)
        value_total = lax.dynamic_update_slice_in_dim(value_total, lax.dynamic_slice_in_dim(value_total, group_start, group_span, 0) + value_part[:group_span], group_start, 0)
        value_total = lax.dynamic_update_slice_in_dim(value_total, lax.dynamic_slice_in_dim(value_total, prev_start, ROWS, 0) + value_part[group_span:], prev_start, 0)
        return ((key_total, value_total), query_part)
    zero_sums = jnp.zeros((TOKENS, KV_HEADS, HD), jnp.float32)
    (key_total, value_total), query_parts = lax.scan(step, (zero_sums, zero_sums), jnp.arange(shard_total, dtype=jnp.int32))
    return (query_parts.reshape(TOKENS, HEADS * HD), key_total.reshape(TOKENS, KV_HEADS * HD), value_total.reshape(TOKENS, KV_HEADS * HD))
```

```python
import functools
import math

import jax
import jax.numpy as jnp
from jax import lax
from jax.experimental import pallas as pl
from jax.experimental.pallas import tpu as pltpu
from jax.sharding import PartitionSpec as P


HD = 128
SCALE = 1.0 / math.sqrt(HD)
LOG2E = 1.4426950408889634
VMEM = pl.BlockSpec(memory_space=pltpu.VMEM)
SMEM = pl.BlockSpec(memory_space=pltpu.SMEM)
HBM = pl.BlockSpec(memory_space=pltpu.HBM)
BF = jnp.bfloat16
F32 = jnp.float32


def passed_along(x, axis, by):
    devices = lax.axis_size(axis)
    return lax.ppermute(x, axis, [(i, (i + by) % devices) for i in range(devices)])


def lanes(start, size):
    return pl.ds(pl.multiple_of(start, 128), size)


def stay(x):
    return pltpu.with_memory_space_constraint(x, pltpu.HBM)


def limit(mib):
    return pltpu.CompilerParams(vmem_limit_bytes=mib << 20)


def pack_kernel(dims, order_hbm, flag_hbm, q_ref, g_ref, k_ref, v_ref, send_ref, kv4_ref, kv_ref, bias_ref, order_ref, flag_ref, sems):
    groups, half, members, outers = dims
    rows = kv_ref.shape[0]
    d = lax.axis_index("dp")
    outer = lax.axis_index("outer")
    member = lax.axis_index("inner")
    wide = groups * half
    moves = [(order_hbm, order_ref), (flag_hbm, flag_ref)]
    for base, ref in ((0, k_ref), (half, v_ref)):
        source = ref.at[:, lanes(d * half, half)]
        moves.append((source, kv_ref.at[:, base : base + half]))
    for g in range(groups):
        away = g * 2 * half + (1 - d) * half
        for base, ref in ((0, q_ref), (wide, g_ref)):
            at = base + g * half
            moves.append((ref.at[:, lanes(away, half)], send_ref.at[:, at : at + half]))
    for base, ref in ((0, k_ref), (half, v_ref)):
        source = ref.at[:, lanes(d * half, half)]
        for c in range(members):
            moves.append((source, kv4_ref.at[c * rows : (c + 1) * rows, base : base + half]))
    copies = [pltpu.make_async_copy(a, b, sems.at[i]) for i, (a, b) in enumerate(moves)]
    for copy in copies:
        copy.start()
    copies[0].wait()
    copies[1].wait()
    shard = outer * members + member
    before = lax.rem(outer + outers - 1, outers) * members + member
    mine = order_ref[shard]
    key_at = lax.broadcasted_iota(jnp.int32, (rows, rows), 0)
    row_at = lax.broadcasted_iota(jnp.int32, (rows, rows), 1)
    triangle = jnp.where(key_at <= row_at, 0.0, -jnp.inf).astype(F32)
    for c in range(members + 1):
        where = outer * members + c if c < members else before
        seen = jnp.logical_and(order_ref[where] < mine, flag_ref[c, shard] == 1)
        flat = jnp.full((rows, rows), jnp.where(seen, 0.0, -jnp.inf), F32)
        if c < members:
            flat = jnp.where(member == c, triangle, flat)
        bias_ref[c * rows : (c + 1) * rows, :] = flat
    for copy in copies[2:]:
        copy.wait()


def attend(q2, g2, keys, values, keys_t, bias2):
    nt = (((1,), (1,)), ((), ()))
    scores = lax.dot_general(keys, q2, nt, preferred_element_type=F32) + bias2
    top = jnp.max(scores, axis=0, keepdims=True)
    exps = jnp.exp2((scores - top) * (SCALE * LOG2E))
    weight_grads = lax.dot_general(values, g2, nt, preferred_element_type=F32)
    inverse = 1.0 / jnp.sum(exps, axis=0, keepdims=True)
    delta = jnp.sum(exps * weight_grads, axis=0, keepdims=True) * inverse
    soft = exps * inverse
    soft_low = soft.astype(BF)
    score_grads = (soft * ((weight_grads - delta) * SCALE)).astype(BF)
    value_part = jnp.dot(soft_low, g2, preferred_element_type=F32)
    key_part = jnp.dot(score_grads, q2, preferred_element_type=F32)
    query_t = jnp.dot(keys_t, score_grads, preferred_element_type=F32)
    return query_t, key_part, value_part


def heads_kernel(local, half, groups, members, *refs):
    if local:
        q_ref, g_ref, kv_ref, prev_ref, bias_ref, dq_ref, dk_ref, dv_ref, keys, values, keys_t = refs
    else:
        (qg_ref, kv_ref, prev_ref, bias_ref, dk_in, dv_in, dq_ref, part_ref, back_ref, keys, values, keys_t, dk_ref, dv_ref) = refs
    rows = prev_ref.shape[0]
    span = members * rows
    per = half // HD
    d = lax.axis_index("dp")
    for j in range(per):
        keys[j, :span, :] = kv_ref[:, j * HD : (j + 1) * HD]
        keys[j, span:, :] = prev_ref[:, j * HD : (j + 1) * HD]
        values[j, :span, :] = kv_ref[:, half + j * HD : half + (j + 1) * HD]
        values[j, span:, :] = prev_ref[:, half + j * HD : half + (j + 1) * HD]
        keys_t[j] = keys[j].T
    pairs = groups // 2

    def step(i, carry):
        j, pair = i // pairs, i % pairs
        wide = groups * half
        if local:
            at = [(2 * pair + e) * 2 * half + d * half + j * HD for e in range(2)]
            q2 = jnp.concatenate([q_ref[:, lanes(a, HD)] for a in at], 0)
            g2 = jnp.concatenate([g_ref[:, lanes(a, HD)] for a in at], 0)
        else:
            at = [(2 * pair + e) * half + j * HD for e in range(2)]
            q2 = jnp.concatenate([qg_ref[:, lanes(a, HD)] for a in at], 0)
            g2 = jnp.concatenate([qg_ref[:, lanes(wide + a, HD)] for a in at], 0)
        bias = bias_ref[...]
        query_t, key_part, value_part = attend(
            q2, g2, keys[j], values[j], keys_t[j], jnp.concatenate([bias, bias], 1)
        )
        for e in range(2):
            out_at = (2 * pair + e) * half + j * HD
            dq_ref[:, lanes(out_at, HD)] = query_t[:, e * rows : (e + 1) * rows].T.astype(BF)
        if local:
            first = pair == 0

            @pl.when(first)
            def _():
                dk_ref[j] = key_part
                dv_ref[j] = value_part

            @pl.when(jnp.logical_not(first))
            def _():
                dk_ref[j] += key_part
                dv_ref[j] += value_part
        else:
            first = pair == 0

            @pl.when(first)
            def _():
                dk_ref[j] = dk_in[j] + key_part
                dv_ref[j] = dv_in[j] + value_part

            @pl.when(jnp.logical_not(first))
            def _():
                dk_ref[j] += key_part
                dv_ref[j] += value_part

        return carry

    lax.fori_loop(0, per * pairs, step, 0)
    if not local:
        for j in range(per):
            for ref, base in ((dk_ref, 0), (dv_ref, half)):
                at = base + j * HD
                part_ref[:, at : at + HD] = ref[j, :span, :].astype(BF)
                back_ref[:, at : at + HD] = ref[j, span:, :].astype(BF)


def finish_kernel(half, groups, members, part_ref, back_ref, own_dq_ref, far_dq_ref, dq_ref, dk_ref, dv_ref):
    rows = back_ref.shape[0]
    d = lax.axis_index("dp")
    for g in range(groups):
        dq_ref[:, lanes(g * 2 * half + d * half, half)] = own_dq_ref[:, g * half : (g + 1) * half]
        dq_ref[:, lanes(g * 2 * half + (1 - d) * half, half)] = far_dq_ref[:, g * half : (g + 1) * half]
    total = back_ref[...].astype(F32)
    for c in range(members):
        total = total + part_ref[c * rows : (c + 1) * rows, :].astype(F32)
    dk_ref[...] = total[:, :half]
    dv_ref[...] = total[:, half:]


def step(queries, out_grad, key_rows, value_rows, block_order, block_flags):
    rows = queries.shape[0]
    key_heads = key_rows.shape[1] // HD
    groups = queries.shape[1] // (key_heads * HD)
    members = lax.axis_size("inner")
    outers = lax.axis_size("outer")
    half = key_heads * HD // lax.axis_size("dp")
    per = half // HD
    window = (members + 1) * rows
    S = jax.ShapeDtypeStruct
    send, kv4, kv, bias = pl.pallas_call(
        functools.partial(pack_kernel, (groups, half, members, outers)),
        out_shape=(
            S((rows, 2 * groups * half), BF),
            S((members * rows, 2 * half), BF),
            S((rows, 2 * half), BF),
            S((window, rows), F32),
        ),
        in_specs=[HBM] * 6,
        out_specs=(VMEM,) * 4,
        scratch_shapes=[
            pltpu.SMEM(block_order.shape, jnp.int32),
            pltpu.SMEM(block_flags.shape[::-1], jnp.int32),
            pltpu.SemaphoreType.DMA((4 + 2 * groups + 2 * members,)),
        ],
        compiler_params=limit(8),
        name="pack",
    )(*[stay(a) for a in (block_order, block_flags.T, queries, out_grad, key_rows, value_rows)])
    prev_kv = passed_along(kv, "outer", 1)
    received = passed_along(send, "dp", 1)
    group_kv = lax.all_to_all(kv4, "inner", 0, 0, tiled=True)
    scratch = [pltpu.VMEM((per, window, HD), BF), pltpu.VMEM((per, window, HD), BF), pltpu.VMEM((per, HD, window), BF)]
    cost = pl.CostEstimate(
        flops=10 * rows * window * HD * groups * per,
        transcendentals=rows * window * groups * per,
        bytes_accessed=4 * rows * window * per * groups,
    )
    own_dq, dk, dv = pl.pallas_call(
        functools.partial(heads_kernel, True, half, groups, members),
        out_shape=(S((rows, groups * half), BF), S((per, window, HD), F32), S((per, window, HD), F32)),
        in_specs=[VMEM] * 5,
        out_specs=(VMEM,) * 3,
        scratch_shapes=scratch,
        cost_estimate=cost,
        compiler_params=limit(24),
        name="own_heads",
    )(queries, out_grad, group_kv, prev_kv, bias)
    far_dq, part, back = pl.pallas_call(
        functools.partial(heads_kernel, False, half, groups, members),
        out_shape=(S((rows, groups * half), BF), S((members * rows, 2 * half), BF), S((rows, 2 * half), BF)),
        in_specs=[VMEM] * 6,
        out_specs=(VMEM,) * 3,
        scratch_shapes=scratch + [pltpu.VMEM((per, window, HD), F32), pltpu.VMEM((per, window, HD), F32)],
        cost_estimate=cost,
        compiler_params=limit(24),
        name="far_heads",
    )(received, group_kv, prev_kv, bias, dk, dv)
    far_dq = passed_along(far_dq, "dp", 1)
    part = lax.all_to_all(part, "inner", 0, 0, tiled=True)
    back = passed_along(back, "outer", -1)
    return pl.pallas_call(
        functools.partial(finish_kernel, half, groups, members),
        out_shape=(S(queries.shape, BF), S((rows, half), F32), S((rows, half), F32)),
        in_specs=[VMEM] * 4,
        out_specs=(VMEM,) * 3,
        compiler_params=limit(8),
        name="finish",
    )(part, back, own_dq, far_dq)


def solution(mesh):
    tokens = P(("outer", "inner"), None)
    split = P(("outer", "inner"), "dp")
    return jax.shard_map(
        step,
        mesh=mesh,
        in_specs=(split, split, tokens, tokens, P(), P()),
        out_specs=(split, split, split),
        check_vma=False,
    )
```

```python
import functools
import math

import jax
import jax.numpy as jnp
from jax import lax
from jax.experimental import pallas as pl
from jax.experimental.pallas import tpu as pltpu
from jax.sharding import PartitionSpec as P


HD = 128
SCALE = 1.0 / math.sqrt(HD)
LOG2E = 1.4426950408889634
VMEM = pl.BlockSpec(memory_space=pltpu.VMEM)
SMEM = pl.BlockSpec(memory_space=pltpu.SMEM)
HBM = pl.BlockSpec(memory_space=pltpu.HBM)
BF = jnp.bfloat16
F32 = jnp.float32


def passed_along(x, axis, by):
    devices = lax.axis_size(axis)
    return lax.ppermute(x, axis, [(i, (i + by) % devices) for i in range(devices)])


def lanes(start, size):
    return pl.ds(pl.multiple_of(start, 128), size)


def stay(x):
    return pltpu.with_memory_space_constraint(x, pltpu.HBM)


def limit(mib):
    return pltpu.CompilerParams(vmem_limit_bytes=mib << 20)


def pack_kernel(dims, order_hbm, flag_hbm, q_ref, g_ref, k_ref, v_ref, send_ref, kv4_ref, kv_ref, bias_ref, order_ref, flag_ref, sems):
    groups, half, members, outers = dims
    rows = kv_ref.shape[0]
    d = lax.axis_index("dp")
    outer = lax.axis_index("outer")
    member = lax.axis_index("inner")
    wide = groups * half
    moves = [(order_hbm, order_ref), (flag_hbm, flag_ref)]
    for base, ref in ((0, k_ref), (half, v_ref)):
        source = ref.at[:, lanes(d * half, half)]
        moves.append((source, kv_ref.at[:, base : base + half]))
    for g in range(groups):
        away = g * 2 * half + (1 - d) * half
        for base, ref in ((0, q_ref), (wide, g_ref)):
            at = base + g * half
            moves.append((ref.at[:, lanes(away, half)], send_ref.at[:, at : at + half]))
    for base, ref in ((0, k_ref), (half, v_ref)):
        source = ref.at[:, lanes(d * half, half)]
        for c in range(members):
            moves.append((source, kv4_ref.at[c * rows : (c + 1) * rows, base : base + half]))
    copies = [pltpu.make_async_copy(a, b, sems.at[i]) for i, (a, b) in enumerate(moves)]
    for copy in copies:
        copy.start()
    copies[0].wait()
    copies[1].wait()
    shard = outer * members + member
    before = lax.rem(outer + outers - 1, outers) * members + member
    mine = order_ref[shard]
    key_at = lax.broadcasted_iota(jnp.int32, (rows, rows), 0)
    row_at = lax.broadcasted_iota(jnp.int32, (rows, rows), 1)
    triangle = jnp.where(key_at <= row_at, 0.0, -jnp.inf).astype(F32)
    for c in range(members + 1):
        where = outer * members + c if c < members else before
        seen = jnp.logical_and(order_ref[where] < mine, flag_ref[c, shard] == 1)
        flat = jnp.full((rows, rows), jnp.where(seen, 0.0, -jnp.inf), F32)
        if c < members:
            flat = jnp.where(member == c, triangle, flat)
        bias_ref[c * rows : (c + 1) * rows, :] = flat
    for copy in copies[2:]:
        copy.wait()


def attend_kernel(half, groups, members, q_ref, g_ref, qg_ref, kv_ref, prev_ref, bias_ref, own_dq, far_dq, part_ref, back_ref, *scratch):
    scores, grads, softs, slopes = scratch[0:2], scratch[2:4], scratch[4:6], scratch[6:8]
    keys_t, key_sum, value_sum = scratch[8:11]
    rows = prev_ref.shape[0]
    slots = members + 1
    per = half // HD
    wide = groups * half
    d = lax.axis_index("dp")
    nt = (((1,), (1,)), ((), ()))
    units = [(j, own, g) for j in range(per) for own in (True, False) for g in range(0, groups, 2)]
    pack = groups // 2

    def chunk(j, c, base):
        if c == members:
            return prev_ref[:, base + j * HD : base + (j + 1) * HD]
        return kv_ref[c * rows : (c + 1) * rows, base + j * HD : base + (j + 1) * HD]

    def heads(i, grad):
        j, own, g = units[i]
        if own:
            ref = g_ref if grad else q_ref
            parts = [ref[:, lanes((g + e) * 2 * half + d * half + j * HD, HD)] for e in range(2)]
        else:
            base = wide if grad else 0
            parts = [qg_ref[:, base + (g + e) * half + j * HD : base + (g + e) * half + (j + 1) * HD] for e in range(2)]
        return jnp.concatenate(parts, 0)

    def fold(x, op):
        return op(x.reshape(x.shape[0] // 8, 8, x.shape[1]), axis=0)

    def stage_a(i):
        j = units[i][0]
        q2, g2 = heads(i, False), heads(i, True)
        top = None
        for c in range(slots):
            at = slice(c * rows, (c + 1) * rows)
            bias = bias_ref[at, :]
            s = lax.dot_general(chunk(j, c, 0), q2, nt, preferred_element_type=F32)
            s = s + jnp.concatenate([bias, bias], 1)
            scores[i % 2][at, :] = s
            peak = fold(s, jnp.max)
            top = peak if top is None else jnp.maximum(top, peak)
        for c in range(slots):
            at = slice(c * rows, (c + 1) * rows)
            grads[i % 2][at, :] = lax.dot_general(chunk(j, c, half), g2, nt, preferred_element_type=F32)
        return jnp.max(top, axis=0, keepdims=True)

    def stage_b(i, top):
        total = delta = None
        for c in range(slots):
            at = slice(c * rows, (c + 1) * rows)
            e = jnp.exp2((scores[i % 2][at, :] - top) * (SCALE * LOG2E))
            scores[i % 2][at, :] = e
            te, de = fold(e, jnp.sum), fold(e * grads[i % 2][at, :], jnp.sum)
            total = te if total is None else total + te
            delta = de if delta is None else delta + de
        inverse = 1.0 / jnp.sum(total, axis=0, keepdims=True)
        delta = jnp.sum(delta, axis=0, keepdims=True) * inverse
        bunch, lane = (i // pack) % 2, (i % pack) * 2 * rows
        for c in range(slots):
            at = slice(c * rows, (c + 1) * rows)
            soft = scores[i % 2][at, :] * inverse
            softs[bunch][at, lane : lane + 2 * rows] = soft.astype(BF)
            slope = soft * ((grads[i % 2][at, :] - delta) * SCALE)
            slopes[bunch][at, lane : lane + 2 * rows] = slope.astype(BF)

    def stage_q(i):
        j, own, g = units[i]
        bunch, lane = (i // pack) % 2, (i % pack) * 2 * rows
        out = jnp.dot(keys_t[j], slopes[bunch][:, lane : lane + 2 * rows], preferred_element_type=F32)
        ref = own_dq if own else far_dq
        for e in range(2):
            at = (g + e) * half + j * HD
            ref[:, at : at + HD] = out[:, e * rows : (e + 1) * rows].T.astype(BF)

    def stage_kv(k, grad):
        first = k * pack
        j, own, _ = units[first]
        other = jnp.concatenate([heads(first + e, grad) for e in range(pack)], 0)
        weights, total, base = (softs, value_sum, half) if grad else (slopes, key_sum, 0)
        for c in range(slots):
            at = slice(c * rows, (c + 1) * rows)
            out = jnp.dot(weights[k % 2][at, :], other, preferred_element_type=F32)
            if own:
                total[at, :] = out
                continue
            out = (total[at, :] + out).astype(BF)
            lane = slice(base + j * HD, base + (j + 1) * HD)
            if c == members:
                back_ref[:, lane] = out
            else:
                part_ref[at, lane] = out

    for j in range(per):
        for c in range(slots):
            keys_t[j, :, c * rows : (c + 1) * rows] = chunk(j, c, 0).T
    count = len(units)
    tops = {}
    for t in range(count + pack + 2):
        if t < count:
            tops[t] = stage_a(t)
        if 0 <= t - 1 < count:
            stage_b(t - 1, tops.pop(t - 1))
        if 0 <= t - 2 < count:
            stage_q(t - 2)
        for lag, grad in ((pack, True), (pack + 1, False)):
            k, rest = divmod(t - lag - 1, pack)
            if rest == 0 and 0 <= k < count // pack:
                stage_kv(k, grad)


def finish_kernel(half, groups, members, part_ref, back_ref, own_dq_ref, far_dq_ref, dq_ref, dk_ref, dv_ref):
    rows = back_ref.shape[0]
    d = lax.axis_index("dp")
    for g in range(groups):
        dq_ref[:, lanes(g * 2 * half + d * half, half)] = own_dq_ref[:, g * half : (g + 1) * half]
        dq_ref[:, lanes(g * 2 * half + (1 - d) * half, half)] = far_dq_ref[:, g * half : (g + 1) * half]
    total = back_ref[...].astype(F32)
    for c in range(members):
        total = total + part_ref[c * rows : (c + 1) * rows, :].astype(F32)
    dk_ref[...] = total[:, :half]
    dv_ref[...] = total[:, half:]


def step(queries, out_grad, key_rows, value_rows, block_order, block_flags):
    rows = queries.shape[0]
    key_heads = key_rows.shape[1] // HD
    groups = queries.shape[1] // (key_heads * HD)
    members = lax.axis_size("inner")
    outers = lax.axis_size("outer")
    half = key_heads * HD // lax.axis_size("dp")
    per = half // HD
    window = (members + 1) * rows
    S = jax.ShapeDtypeStruct
    send, kv4, kv, bias = pl.pallas_call(
        functools.partial(pack_kernel, (groups, half, members, outers)),
        out_shape=(
            S((rows, 2 * groups * half), BF),
            S((members * rows, 2 * half), BF),
            S((rows, 2 * half), BF),
            S((window, rows), F32),
        ),
        in_specs=[HBM] * 6,
        out_specs=(VMEM,) * 4,
        scratch_shapes=[
            pltpu.SMEM(block_order.shape, jnp.int32),
            pltpu.SMEM(block_flags.shape[::-1], jnp.int32),
            pltpu.SemaphoreType.DMA((4 + 2 * groups + 2 * members,)),
        ],
        compiler_params=limit(8),
        name="pack",
    )(*[stay(a) for a in (block_order, block_flags.T, queries, out_grad, key_rows, value_rows)])
    prev_kv = passed_along(kv, "outer", 1)
    received = passed_along(send, "dp", 1)
    group_kv = lax.all_to_all(kv4, "inner", 0, 0, tiled=True)
    cost = pl.CostEstimate(
        flops=20 * rows * window * HD * groups * per,
        transcendentals=2 * rows * window * groups * per,
        bytes_accessed=8 * rows * window * per * groups,
    )
    own_dq, far_dq, part, back = pl.pallas_call(
        functools.partial(attend_kernel, half, groups, members),
        out_shape=(
            S((rows, groups * half), BF),
            S((rows, groups * half), BF),
            S((members * rows, 2 * half), BF),
            S((rows, 2 * half), BF),
        ),
        in_specs=[VMEM] * 6,
        out_specs=(VMEM,) * 4,
        scratch_shapes=[pltpu.VMEM((window, 2 * rows), F32)] * 4
        + [pltpu.VMEM((window, groups * rows), BF)] * 4
        + [pltpu.VMEM((per, HD, window), BF), pltpu.VMEM((window, HD), F32), pltpu.VMEM((window, HD), F32)],
        cost_estimate=cost,
        compiler_params=limit(24),
        name="attend",
    )(queries, out_grad, received, group_kv, prev_kv, bias)
    far_dq = passed_along(far_dq, "dp", 1)
    part = lax.all_to_all(part, "inner", 0, 0, tiled=True)
    back = passed_along(back, "outer", -1)
    return pl.pallas_call(
        functools.partial(finish_kernel, half, groups, members),
        out_shape=(S(queries.shape, BF), S((rows, half), F32), S((rows, half), F32)),
        in_specs=[VMEM] * 4,
        out_specs=(VMEM,) * 3,
        compiler_params=limit(8),
        name="finish",
    )(part, back, own_dq, far_dq)


def solution(mesh):
    tokens = P(("outer", "inner"), None)
    split = P(("outer", "inner"), "dp")
    return jax.shard_map(
        step,
        mesh=mesh,
        in_specs=(split, split, tokens, tokens, P(), P()),
        out_specs=(split, split, split),
        check_vma=False,
    )
```

```python
import functools
import math

import jax
import jax.numpy as jnp
from jax import lax
from jax.experimental import pallas as pl
from jax.experimental.pallas import tpu as pltpu
from jax.sharding import PartitionSpec as P


HD = 128
SCALE = 1.0 / math.sqrt(HD)
LOG2E = 1.4426950408889634
VMEM = pl.BlockSpec(memory_space=pltpu.VMEM)
SMEM = pl.BlockSpec(memory_space=pltpu.SMEM)
HBM = pl.BlockSpec(memory_space=pltpu.HBM)
BF = jnp.bfloat16
F32 = jnp.float32


def passed_along(x, axis, by):
    devices = lax.axis_size(axis)
    return lax.ppermute(x, axis, [(i, (i + by) % devices) for i in range(devices)])


def lanes(start, size):
    return pl.ds(pl.multiple_of(start, 128), size)


def stay(x):
    return pltpu.with_memory_space_constraint(x, pltpu.HBM)


def limit(mib):
    return pltpu.CompilerParams(vmem_limit_bytes=mib << 20)


def pack_kernel(dims, order_hbm, flag_hbm, q_ref, g_ref, k_ref, v_ref, send_ref, kv4_ref, kv_ref, bias_ref, order_ref, flag_ref, sems):
    groups, half, members, outers = dims
    rows = kv_ref.shape[0]
    d = lax.axis_index("dp")
    outer = lax.axis_index("outer")
    member = lax.axis_index("inner")
    wide = groups * half
    moves = [(order_hbm, order_ref), (flag_hbm, flag_ref)]
    for base, ref in ((0, k_ref), (half, v_ref)):
        source = ref.at[:, lanes(d * half, half)]
        moves.append((source, kv_ref.at[:, base : base + half]))
    for g in range(groups):
        away = g * 2 * half + (1 - d) * half
        for base, ref in ((0, q_ref), (wide, g_ref)):
            at = base + g * half
            moves.append((ref.at[:, lanes(away, half)], send_ref.at[:, at : at + half]))
    for c in range(members):
        moves.append((kv_ref, kv4_ref.at[c * rows : (c + 1) * rows, :]))
    copies = [pltpu.make_async_copy(a, b, sems.at[i]) for i, (a, b) in enumerate(moves)]
    for copy in copies[:-members]:
        copy.start()
    copies[2].wait()
    copies[3].wait()
    for copy in copies[-members:]:
        copy.start()
    copies[0].wait()
    copies[1].wait()
    shard = outer * members + member
    before = lax.rem(outer + outers - 1, outers) * members + member
    mine = order_ref[shard]
    key_at = lax.broadcasted_iota(jnp.int32, (rows, rows), 0)
    row_at = lax.broadcasted_iota(jnp.int32, (rows, rows), 1)
    triangle = jnp.where(key_at <= row_at, 0.0, -jnp.inf).astype(F32)
    for c in range(members + 1):
        where = outer * members + c if c < members else before
        seen = jnp.logical_and(order_ref[where] < mine, flag_ref[c, shard] == 1)
        flat = jnp.full((rows, rows), jnp.where(seen, 0.0, -jnp.inf), F32)
        if c < members:
            flat = jnp.where(member == c, triangle, flat)
        bias_ref[c * rows : (c + 1) * rows, :] = flat
    for copy in copies[4:]:
        copy.wait()


def attend_kernel(half, groups, members, q_ref, g_ref, qg_ref, kv_ref, prev_ref, bias_ref, own_dq, far_dq, part_ref, back_ref, *scratch):
    scores, grads, softs, slopes = scratch[0:2], scratch[2:4], scratch[4:6], scratch[6:8]
    keys_t, key_sum, value_sum, part_vmem, sems = scratch[8:13]
    copies = []
    rows = prev_ref.shape[0]
    slots = members + 1
    per = half // HD
    wide = groups * half
    d = lax.axis_index("dp")
    nt = (((1,), (1,)), ((), ()))
    units = [(j, own, g) for j in range(per) for own in (True, False) for g in range(0, groups, 2)]
    pack = groups // 2

    def chunk(j, c, base):
        if c == members:
            return prev_ref[:, base + j * HD : base + (j + 1) * HD]
        return kv_ref[c * rows : (c + 1) * rows, base + j * HD : base + (j + 1) * HD]

    def heads(i, grad):
        j, own, g = units[i]
        if own:
            ref = g_ref if grad else q_ref
            parts = [ref[:, lanes((g + e) * 2 * half + d * half + j * HD, HD)] for e in range(2)]
        else:
            base = wide if grad else 0
            parts = [qg_ref[:, base + (g + e) * half + j * HD : base + (g + e) * half + (j + 1) * HD] for e in range(2)]
        return jnp.concatenate(parts, 0)

    def fold(x, op):
        return op(x.reshape(x.shape[0] // 8, 8, x.shape[1]), axis=0)

    def stage_a(i):
        j = units[i][0]
        q2, g2 = heads(i, False), heads(i, True)
        span = members * rows
        tops = []
        for at, ref in ((slice(0, span), kv_ref), (slice(span, span + rows), prev_ref)):
            bias = bias_ref[at, :]
            s = lax.dot_general(ref[:, j * HD : (j + 1) * HD], q2, nt, preferred_element_type=F32)
            s = s + jnp.concatenate([bias, bias], 1)
            scores[i % 2][at, :] = s
            tops.append(fold(s, jnp.max))
            lane = slice(half + j * HD, half + (j + 1) * HD)
            grads[i % 2][at, :] = lax.dot_general(ref[:, lane], g2, nt, preferred_element_type=F32)
        return jnp.max(jnp.maximum(*tops), axis=0, keepdims=True)

    def stage_b(i, top):
        total = delta = None
        for c in range(slots):
            at = slice(c * rows, (c + 1) * rows)
            e = jnp.exp2((scores[i % 2][at, :] - top) * (SCALE * LOG2E))
            scores[i % 2][at, :] = e
            te, de = fold(e, jnp.sum), fold(e * grads[i % 2][at, :], jnp.sum)
            total = te if total is None else total + te
            delta = de if delta is None else delta + de
        inverse = 1.0 / jnp.sum(total, axis=0, keepdims=True)
        delta = jnp.sum(delta, axis=0, keepdims=True) * inverse
        bunch, lane = (i // pack) % 2, (i % pack) * 2 * rows
        for c in range(slots):
            at = slice(c * rows, (c + 1) * rows)
            soft = scores[i % 2][at, :] * inverse
            softs[bunch][at, lane : lane + 2 * rows] = soft.astype(BF)
            slope = soft * ((grads[i % 2][at, :] - delta) * SCALE)
            slopes[bunch][at, lane : lane + 2 * rows] = slope.astype(BF)

    def stage_q(i):
        j, own, g = units[i]
        bunch, lane = (i // pack) % 2, (i % pack) * 2 * rows
        out = jnp.dot(keys_t[j], slopes[bunch][:, lane : lane + 2 * rows], preferred_element_type=F32)
        ref = own_dq if own else far_dq
        for e in range(2):
            at = (g + e) * half + j * HD
            ref[:, at : at + HD] = out[:, e * rows : (e + 1) * rows].T.astype(BF)

    def stage_kv(k, grad):
        first = k * pack
        j, own, _ = units[first]
        other = jnp.concatenate([heads(first + e, grad) for e in range(pack)], 0)
        weights, total, base = (softs, value_sum, half) if grad else (slopes, key_sum, 0)
        out = jnp.dot(weights[k % 2][...], other, preferred_element_type=F32)
        if own:
            total[...] = out
            return
        out = (total[...] + out).astype(BF)
        lane = slice(base + j * HD, base + (j + 1) * HD)
        part_vmem[:, lane] = out[: members * rows]
        back_ref[:, lane] = out[members * rows :]
        copies.append(pltpu.make_async_copy(part_vmem.at[:, lane], part_ref.at[:, lane], sems.at[len(copies)]))
        copies[-1].start()

    for j in range(per):
        for c in range(slots):
            at = slice(c * rows, (c + 1) * rows)
            keys_t[j, :, at] = chunk(j, c, 0).T
    count = len(units)
    tops = {}
    for t in range(count + pack + 2):
        if 0 <= t - 1 < count:
            stage_b(t - 1, tops.pop(t - 1))
        if t < count:
            tops[t] = stage_a(t)
        for lag, grad in ((pack, True), (pack + 1, False)):
            k, rest = divmod(t - lag - 1, pack)
            if rest == 0 and 0 <= k < count // pack:
                stage_kv(k, grad)
        if 0 <= t - 2 < count:
            stage_q(t - 2)
    for copy in copies:
        copy.wait()


def finish_kernel(half, groups, members, part_ref, back_ref, own_dq_ref, far_dq_ref, dq_ref, dk_ref, dv_ref):
    rows = back_ref.shape[0]
    d = lax.axis_index("dp")
    for g in range(groups):
        dq_ref[:, lanes(g * 2 * half + d * half, half)] = own_dq_ref[:, g * half : (g + 1) * half]
        dq_ref[:, lanes(g * 2 * half + (1 - d) * half, half)] = far_dq_ref[:, g * half : (g + 1) * half]
    total = back_ref[...].astype(F32)
    for c in range(members):
        total = total + part_ref[c * rows : (c + 1) * rows, :].astype(F32)
    dk_ref[...] = total[:, :half]
    dv_ref[...] = total[:, half:]


def step(queries, out_grad, key_rows, value_rows, block_order, block_flags):
    rows = queries.shape[0]
    key_heads = key_rows.shape[1] // HD
    groups = queries.shape[1] // (key_heads * HD)
    members = lax.axis_size("inner")
    outers = lax.axis_size("outer")
    half = key_heads * HD // lax.axis_size("dp")
    per = half // HD
    window = (members + 1) * rows
    S = jax.ShapeDtypeStruct
    send, kv4, kv, bias = pl.pallas_call(
        functools.partial(pack_kernel, (groups, half, members, outers)),
        out_shape=(
            S((rows, 2 * groups * half), BF),
            S((members * rows, 2 * half), BF),
            S((rows, 2 * half), BF),
            S((window, rows), F32),
        ),
        in_specs=[HBM] * 6,
        out_specs=(VMEM, HBM, VMEM, VMEM),
        scratch_shapes=[
            pltpu.SMEM(block_order.shape, jnp.int32),
            pltpu.SMEM(block_flags.shape[::-1], jnp.int32),
            pltpu.SemaphoreType.DMA((4 + 2 * groups + members,)),
        ],
        compiler_params=limit(8),
        name="pack",
    )(*[stay(a) for a in (block_order, block_flags.T, queries, out_grad, key_rows, value_rows)])
    prev_kv = passed_along(kv, "outer", 1)
    received = passed_along(send, "dp", 1)
    group_kv = lax.all_to_all(kv4, "inner", 0, 0, tiled=True)
    cost = pl.CostEstimate(
        flops=20 * rows * window * HD * groups * per,
        transcendentals=2 * rows * window * groups * per,
        bytes_accessed=8 * rows * window * per * groups,
    )
    own_dq, far_dq, part, back = pl.pallas_call(
        functools.partial(attend_kernel, half, groups, members),
        out_shape=(
            S((rows, groups * half), BF),
            S((rows, groups * half), BF),
            S((members * rows, 2 * half), BF),
            S((rows, 2 * half), BF),
        ),
        in_specs=[VMEM] * 6,
        out_specs=(VMEM, VMEM, HBM, VMEM),
        scratch_shapes=[pltpu.VMEM((window, 2 * rows), F32)] * 4
        + [pltpu.VMEM((window, groups * rows), BF)] * 4
        + [pltpu.VMEM((per, HD, window), BF), pltpu.VMEM((window, HD), F32), pltpu.VMEM((window, HD), F32)]
        + [pltpu.VMEM((members * rows, 2 * half), BF), pltpu.SemaphoreType.DMA((2 * per,))],
        cost_estimate=cost,
        compiler_params=pltpu.CompilerParams(vmem_limit_bytes=24 << 20),
        name="attend",
    )(queries, out_grad, received, group_kv, prev_kv, bias)
    far_dq = passed_along(far_dq, "dp", 1)
    part = lax.all_to_all(part, "inner", 0, 0, tiled=True)
    back = passed_along(back, "outer", -1)
    return pl.pallas_call(
        functools.partial(finish_kernel, half, groups, members),
        out_shape=(S(queries.shape, BF), S((rows, half), F32), S((rows, half), F32)),
        in_specs=[VMEM] * 4,
        out_specs=(VMEM,) * 3,
        compiler_params=limit(8),
        name="finish",
    )(part, back, own_dq, far_dq)


def solution(mesh):
    tokens = P(("outer", "inner"), None)
    split = P(("outer", "inner"), "dp")
    return jax.shard_map(
        step,
        mesh=mesh,
        in_specs=(split, split, tokens, tokens, P(), P()),
        out_specs=(split, split, split),
        check_vma=False,
    )
```

```python
import functools
import math

import jax
import jax.numpy as jnp
from jax import lax
from jax.experimental import pallas as pl
from jax.experimental.pallas import tpu as pltpu
from jax.sharding import PartitionSpec as P


HD = 128
SCALE = 1.0 / math.sqrt(HD)
LOG2E = 1.4426950408889634
VMEM = pl.BlockSpec(memory_space=pltpu.VMEM)
SMEM = pl.BlockSpec(memory_space=pltpu.SMEM)
HBM = pl.BlockSpec(memory_space=pltpu.HBM)
BF = jnp.bfloat16
F32 = jnp.float32


def passed_along(x, axis, by):
    devices = lax.axis_size(axis)
    return lax.ppermute(x, axis, [(i, (i + by) % devices) for i in range(devices)])


def lanes(start, size):
    return pl.ds(pl.multiple_of(start, 128), size)


def stay(x):
    return pltpu.with_memory_space_constraint(x, pltpu.HBM)


def limit(mib):
    return pltpu.CompilerParams(vmem_limit_bytes=mib << 20)


def pack_kernel(dims, order_hbm, flag_hbm, q_ref, g_ref, k_ref, v_ref, send_ref, kv_ref, bias_ref, order_ref, flag_ref, sems):
    groups, half, members, outers = dims
    rows = kv_ref.shape[0]
    d = lax.axis_index("dp")
    outer = lax.axis_index("outer")
    member = lax.axis_index("inner")
    wide = groups * half
    moves = [(order_hbm, order_ref), (flag_hbm, flag_ref)]
    for base, ref in ((0, k_ref), (half, v_ref)):
        source = ref.at[:, lanes(d * half, half)]
        moves.append((source, kv_ref.at[:, base : base + half]))
    for g in range(groups):
        away = g * 2 * half + (1 - d) * half
        for base, ref in ((0, q_ref), (wide, g_ref)):
            at = base + g * half
            moves.append((ref.at[:, lanes(away, half)], send_ref.at[:, at : at + half]))
    copies = [pltpu.make_async_copy(a, b, sems.at[i]) for i, (a, b) in enumerate(moves)]
    for copy in copies:
        copy.start()
    copies[0].wait()
    copies[1].wait()
    shard = outer * members + member
    before = lax.rem(outer + outers - 1, outers) * members + member
    mine = order_ref[shard]
    key_at = lax.broadcasted_iota(jnp.int32, (rows, rows), 0)
    row_at = lax.broadcasted_iota(jnp.int32, (rows, rows), 1)
    triangle = jnp.where(key_at <= row_at, 0.0, -jnp.inf).astype(F32)
    for c in range(members + 1):
        where = outer * members + c if c < members else before
        seen = jnp.logical_and(order_ref[where] < mine, flag_ref[c, shard] == 1)
        flat = jnp.full((rows, rows), jnp.where(seen, 0.0, -jnp.inf), F32)
        if c < members:
            flat = jnp.where(member == c, triangle, flat)
        bias_ref[c * rows : (c + 1) * rows, :] = flat
    for copy in copies[2:]:
        copy.wait()


def spread_kernel(members, kv_ref, kv4_ref, sems):
    rows = kv_ref.shape[0]
    copies = [
        pltpu.make_async_copy(kv_ref, kv4_ref.at[c * rows : (c + 1) * rows, :], sems.at[c]) for c in range(members)
    ]
    for copy in copies:
        copy.start()
    for copy in copies:
        copy.wait()


def attend_kernel(half, groups, members, q_ref, g_ref, qg_ref, kv_ref, prev_ref, bias_ref, own_dq, far_dq, part_ref, back_ref, *scratch):
    scores, grads, softs, slopes = scratch[0:2], scratch[2:4], scratch[4:6], scratch[6:8]
    keys_t, key_sum, value_sum, part_vmem, sems = scratch[8:13]
    copies = []
    rows = prev_ref.shape[0]
    slots = members + 1
    per = half // HD
    wide = groups * half
    d = lax.axis_index("dp")
    nt = (((1,), (1,)), ((), ()))
    units = [(j, own, g) for j in range(per) for own in (True, False) for g in range(0, groups, 2)]
    pack = groups // 2

    def chunk(j, c, base):
        if c == members:
            return prev_ref[:, base + j * HD : base + (j + 1) * HD]
        return kv_ref[c * rows : (c + 1) * rows, base + j * HD : base + (j + 1) * HD]

    def heads(i, grad):
        j, own, g = units[i]
        if own:
            ref = g_ref if grad else q_ref
            parts = [ref[:, lanes((g + e) * 2 * half + d * half + j * HD, HD)] for e in range(2)]
        else:
            base = wide if grad else 0
            parts = [qg_ref[:, base + (g + e) * half + j * HD : base + (g + e) * half + (j + 1) * HD] for e in range(2)]
        return jnp.concatenate(parts, 0)

    def fold(x, op):
        return op(x.reshape(x.shape[0] // 8, 8, x.shape[1]), axis=0)

    def stage_a(i):
        j = units[i][0]
        q2, g2 = heads(i, False), heads(i, True)
        span = members * rows
        tops = []
        for at, ref in ((slice(0, span), kv_ref), (slice(span, span + rows), prev_ref)):
            bias = bias_ref[at, :]
            s = lax.dot_general(ref[:, j * HD : (j + 1) * HD], q2, nt, preferred_element_type=F32)
            s = s + jnp.concatenate([bias, bias], 1)
            scores[i % 2][at, :] = s
            tops.append(fold(s, jnp.max))
            lane = slice(half + j * HD, half + (j + 1) * HD)
            grads[i % 2][at, :] = lax.dot_general(ref[:, lane], g2, nt, preferred_element_type=F32)
        return jnp.max(jnp.maximum(*tops), axis=0, keepdims=True)

    def stage_b(i, top):
        total = delta = None
        for c in range(slots):
            at = slice(c * rows, (c + 1) * rows)
            e = jnp.exp2((scores[i % 2][at, :] - top) * (SCALE * LOG2E))
            scores[i % 2][at, :] = e
            te, de = fold(e, jnp.sum), fold(e * grads[i % 2][at, :], jnp.sum)
            total = te if total is None else total + te
            delta = de if delta is None else delta + de
        inverse = 1.0 / jnp.sum(total, axis=0, keepdims=True)
        delta = jnp.sum(delta, axis=0, keepdims=True) * inverse
        bunch, lane = (i // pack) % 2, (i % pack) * 2 * rows
        for c in range(slots):
            at = slice(c * rows, (c + 1) * rows)
            soft = scores[i % 2][at, :] * inverse
            softs[bunch][at, lane : lane + 2 * rows] = soft.astype(BF)
            slope = soft * ((grads[i % 2][at, :] - delta) * SCALE)
            slopes[bunch][at, lane : lane + 2 * rows] = slope.astype(BF)

    def stage_q(i):
        j, own, g = units[i]
        bunch, lane = (i // pack) % 2, (i % pack) * 2 * rows
        out = jnp.dot(keys_t[j], slopes[bunch][:, lane : lane + 2 * rows], preferred_element_type=F32)
        ref = own_dq if own else far_dq
        for e in range(2):
            at = (g + e) * half + j * HD
            ref[:, at : at + HD] = out[:, e * rows : (e + 1) * rows].T.astype(BF)

    def stage_kv(k, grad):
        first = k * pack
        j, own, _ = units[first]
        other = jnp.concatenate([heads(first + e, grad) for e in range(pack)], 0)
        weights, total, base = (softs, value_sum, half) if grad else (slopes, key_sum, 0)
        out = jnp.dot(weights[k % 2][...], other, preferred_element_type=F32)
        if own:
            total[...] = out
            return
        out = (total[...] + out).astype(BF)
        lane = slice(base + j * HD, base + (j + 1) * HD)
        part_vmem[:, lane] = out[: members * rows]
        back_ref[:, lane] = out[members * rows :]
        copies.append(pltpu.make_async_copy(part_vmem.at[:, lane], part_ref.at[:, lane], sems.at[len(copies)]))
        copies[-1].start()

    for j in range(per):
        for c in range(slots):
            at = slice(c * rows, (c + 1) * rows)
            keys_t[j, :, at] = chunk(j, c, 0).T
    count = len(units)
    tops = {}
    for t in range(count + pack + 2):
        if 0 <= t - 1 < count:
            stage_b(t - 1, tops.pop(t - 1))
        if t < count:
            tops[t] = stage_a(t)
        for lag, grad in ((pack, True), (pack + 1, False)):
            k, rest = divmod(t - lag - 1, pack)
            if rest == 0 and 0 <= k < count // pack:
                stage_kv(k, grad)
        if 0 <= t - 2 < count:
            stage_q(t - 2)
    for copy in copies:
        copy.wait()


def finish_kernel(half, groups, members, part_ref, back_ref, own_dq_ref, far_dq_ref, dq_ref, dk_ref, dv_ref):
    rows = back_ref.shape[0]
    d = lax.axis_index("dp")
    for g in range(groups):
        dq_ref[:, lanes(g * 2 * half + d * half, half)] = own_dq_ref[:, g * half : (g + 1) * half]
        dq_ref[:, lanes(g * 2 * half + (1 - d) * half, half)] = far_dq_ref[:, g * half : (g + 1) * half]
    total = back_ref[...].astype(F32)
    for c in range(members):
        total = total + part_ref[c * rows : (c + 1) * rows, :].astype(F32)
    dk_ref[...] = total[:, :half]
    dv_ref[...] = total[:, half:]


def step(queries, out_grad, key_rows, value_rows, block_order, block_flags):
    rows = queries.shape[0]
    key_heads = key_rows.shape[1] // HD
    groups = queries.shape[1] // (key_heads * HD)
    members = lax.axis_size("inner")
    outers = lax.axis_size("outer")
    half = key_heads * HD // lax.axis_size("dp")
    per = half // HD
    window = (members + 1) * rows
    S = jax.ShapeDtypeStruct
    send, kv, bias = pl.pallas_call(
        functools.partial(pack_kernel, (groups, half, members, outers)),
        out_shape=(
            S((rows, 2 * groups * half), BF),
            S((rows, 2 * half), BF),
            S((window, rows), F32),
        ),
        in_specs=[HBM] * 6,
        out_specs=(VMEM,) * 3,
        scratch_shapes=[
            pltpu.SMEM(block_order.shape, jnp.int32),
            pltpu.SMEM(block_flags.shape[::-1], jnp.int32),
            pltpu.SemaphoreType.DMA((4 + 2 * groups,)),
        ],
        compiler_params=limit(8),
        name="pack",
    )(*[stay(a) for a in (block_order, block_flags.T, queries, out_grad, key_rows, value_rows)])
    prev_kv = passed_along(kv, "outer", 1)
    received = passed_along(send, "dp", 1)
    kv4 = pl.pallas_call(
        functools.partial(spread_kernel, members),
        out_shape=S((members * rows, 2 * half), BF),
        in_specs=[VMEM],
        out_specs=HBM,
        scratch_shapes=[pltpu.SemaphoreType.DMA((members,))],
        compiler_params=limit(4),
        name="spread",
    )(kv)
    group_kv = lax.all_to_all(kv4, "inner", 0, 0, tiled=True)
    cost = pl.CostEstimate(
        flops=20 * rows * window * HD * groups * per,
        transcendentals=2 * rows * window * groups * per,
        bytes_accessed=8 * rows * window * per * groups,
    )
    own_dq, far_dq, part, back = pl.pallas_call(
        functools.partial(attend_kernel, half, groups, members),
        out_shape=(
            S((rows, groups * half), BF),
            S((rows, groups * half), BF),
            S((members * rows, 2 * half), BF),
            S((rows, 2 * half), BF),
        ),
        in_specs=[VMEM] * 6,
        out_specs=(VMEM, VMEM, HBM, VMEM),
        scratch_shapes=[pltpu.VMEM((window, 2 * rows), F32)] * 4
        + [pltpu.VMEM((window, groups * rows), BF)] * 4
        + [pltpu.VMEM((per, HD, window), BF), pltpu.VMEM((window, HD), F32), pltpu.VMEM((window, HD), F32)]
        + [pltpu.VMEM((members * rows, 2 * half), BF), pltpu.SemaphoreType.DMA((2 * per,))],
        cost_estimate=cost,
        compiler_params=pltpu.CompilerParams(vmem_limit_bytes=24 << 20),
        name="attend",
    )(queries, out_grad, received, group_kv, prev_kv, bias)
    far_dq = passed_along(far_dq, "dp", 1)
    part = lax.all_to_all(part, "inner", 0, 0, tiled=True)
    back = passed_along(back, "outer", -1)
    return pl.pallas_call(
        functools.partial(finish_kernel, half, groups, members),
        out_shape=(S(queries.shape, BF), S((rows, half), F32), S((rows, half), F32)),
        in_specs=[VMEM] * 4,
        out_specs=(VMEM,) * 3,
        compiler_params=limit(8),
        name="finish",
    )(part, back, own_dq, far_dq)


def solution(mesh):
    tokens = P(("outer", "inner"), None)
    split = P(("outer", "inner"), "dp")
    return jax.shard_map(
        step,
        mesh=mesh,
        in_specs=(split, split, tokens, tokens, P(), P()),
        out_specs=(split, split, split),
        check_vma=False,
    )
```
